32 devices in a mesh: grp: 2 (over core), tile: 16 (over z, y, x).
Axes of the slice: x: 2, y: 2, z: 4, core: 2. Of those that a mesh axis runs over, the one named last changes fastest.
Arguments:
- basis: bfloat16 [32, 5, 64, 16, 128], P(None, None, 'tile'), may hold values from -18 to 18
- snapshots: bfloat16 [2, 4, 64, 16, 128], P('grp', None, 'tile'), may hold values from -1.5 to 1.5
- coupling: float32 [5, 5], replicated, may hold values from -2.5 to 2.5
Outputs:
- new_vector: float32 [2, 5, 64, 16, 128], P('grp', None, 'tile')
- coefficients: float32 [2, 32], P('grp')
- norms: float32 [2], P('grp')
The draws below stay inside these ranges and needn't reach their ends.
All inputs are finite; a program needn't handle non-finite values.
Results may differ from the reference program's by a relative error of at most 0.0003.
Values may be sent and summed in bfloat16 or wider, within the bound.
A program may use at most 64 MiB of HBM per device.

```python
import jax
import jax.numpy as jnp
from jax import lax

NY = 16
NZ = 128
KRYLOV = 32
NX = 64
STEPS = 2
N_GRP = 2


def draw_basis(key, part):
    extent = (KRYLOV, 5, NX, NY, NZ)
    position = jnp.arange(NX, dtype=jnp.float32).reshape(1, 1, NX, 1, 1) / max(NX - 1, 1)
    values = jnp.clip(jax.random.normal(key, extent, jnp.float32), -6.0, 6.0) * jnp.exp(jnp.log(3.0) * position)
    return values.astype(jnp.bfloat16)


def levels(own_key, dims, pieces, least, high):
    level = 1.0
    for axis_at, parts in pieces:
        draws = jax.random.uniform(jax.random.fold_in(jax.random.fold_in(own_key, 6), axis_at), (parts,), jnp.float32, least / len(pieces), high / len(pieces))
        level = level * jnp.repeat(jnp.exp(draws), dims[axis_at] // parts).reshape((-1,) + (1,) * (len(dims) - 1 - axis_at))
    return level


def noise(stream_key, dims, width, reach, kind=jnp.bfloat16):
    values = width * jax.random.normal(stream_key, dims, jnp.float32)
    return jnp.clip(values, min=-reach, max=reach).astype(kind)


def setup_inputs(seed: int = 0) -> dict:
    key_list = jax.random.split(jax.random.key(seed), 4)
    basis = draw_basis(jax.random.fold_in(key_list[3], 71), 0)
    snapshots = jnp.clip(jax.random.uniform(key_list[1], (STEPS, 4, NX, NY, NZ), jnp.float32, -1.5, 1.5) * levels(key_list[1], (STEPS, 4, NX, NY, NZ), ((0, 2), (2, 16)), -0.4, 0.0), -1.5, 1.5).astype(jnp.bfloat16)
    coupling = noise(key_list[2], (5, 5), 5 ** -0.5, 2.5, jnp.float32)
    return {"basis": basis, "snapshots": snapshots, "coupling": coupling}


viscosity = 0.5
time_step = 0.3

def tendency(extended, base, coupling):
    center = extended[:, 1:-1]
    slope_x = 0.5 * (extended[:, 2:] - extended[:, :-2])
    walled = jnp.pad(center, ((0, 0), (0, 0), (1, 1), (0, 0)))
    upper_y = walled[:, :, 2:]
    lower_y = walled[:, :, :-2]
    slope_y = 0.5 * (upper_y - lower_y)
    upper_z = jnp.roll(center, -1, axis=3)
    lower_z = jnp.roll(center, 1, axis=3)
    slope_z = 0.5 * (upper_z - lower_z)
    laplace = extended[:, 2:] + extended[:, :-2] + upper_y + lower_y + upper_z + lower_z - 6.0 * center
    advect = base[0] * slope_x + base[1] * slope_y + base[2] * slope_z
    coupled = jnp.einsum('kj,jxyz->kxyz', coupling, center, precision=lax.Precision.HIGHEST)
    return viscosity * laplace - advect - base[3] * coupled

def periodic(field):
    return jnp.concatenate([field[:, -1:], field, field[:, :1]], axis=1)

def runge_kutta(state, base, coupling):
    first = state + time_step * tendency(periodic(state), base, coupling)
    second = 0.75 * state + 0.25 * (first + time_step * tendency(periodic(first), base, coupling))
    return state / 3.0 + 2.0 / 3.0 * (second + time_step * tendency(periodic(second), base, coupling))

def project(basis, field, count):
    return lax.map(lambda vector: jnp.sum(vector.astype(jnp.float32) * field) / count, basis)

def expand(basis, weights, field):

    def accumulate(total, pair):
        vector, weight = pair
        return (total - weight * vector.astype(jnp.float32), None)
    result, unused = lax.scan(accumulate, field, (basis, weights))
    return result

def reference(basis, snapshots, coupling):
    krylov = basis.shape[0]
    count = jnp.float32(basis[0].size)
    outputs = []
    coefs = []
    norm_list = []
    for member in range(N_GRP):
        state = basis[krylov - N_GRP + member].astype(jnp.float32)
        for step_index in range(snapshots.shape[0]):
            state = runge_kutta(state, snapshots[step_index].astype(jnp.float32), coupling)
        first_coef = project(basis, state, count)
        first_left = expand(basis, first_coef, state)
        second_coef = project(basis, first_left, count)
        second_left = expand(basis, second_coef, first_left)
        norm_value = jnp.sqrt(jnp.sum(second_left * second_left) / count)
        outputs.append(second_left / norm_value)
        coefs.append(first_coef + second_coef)
        norm_list.append(norm_value)
    return (jnp.stack(outputs), jnp.stack(coefs), jnp.stack(norm_list))
```

```python
import functools

import jax
import jax.numpy as jnp
from jax import lax
from jax.experimental import pallas as pl
from jax.experimental.pallas import tpu as pltpu
from jax.sharding import PartitionSpec as P

viscosity = 0.5
time_step = 0.3
f32 = jnp.float32
bf16 = jnp.bfloat16
MESH = pl.DeviceIdType.MESH
HIGHEST = lax.Precision.HIGHEST


def spans(slab, rim):
    found = {}
    reach = -(-rim // slab)
    for d in range(1, reach + 1):
        width = min(slab, rim - (d - 1) * slab)
        found[-d] = (slab - width, slab)
        found[d] = (0, width)
    return found


def stage(src, old, dst, snap, step, coupling, lo, hi, keep, gain):
    rows, lanes = src.shape[2], src.shape[3]
    row = lax.broadcasted_iota(jnp.int32, (rows, lanes), 0)
    first = row == 0
    last = row == rows - 1
    step_gain = time_step * gain
    mix = [[coupling[k, j] for j in range(5)] for k in range(5)]

    def body(i, carry):
        p = lo + i
        base = [snap[step, n, p].astype(f32) for n in range(4)]
        half = [(0.5 * step_gain) * base[n] for n in range(3)]
        edge = viscosity * step_gain
        x_up, x_low = edge - half[0], edge + half[0]
        y_up = jnp.where(last, 0.0, edge - half[1])
        y_low = jnp.where(first, 0.0, edge + half[1])
        z_up, z_low = edge - half[2], edge + half[2]
        pull = step_gain * base[3]
        center = [src[k, p] for k in range(5)]
        own = gain - 6.0 * viscosity * step_gain
        for k in range(5):
            q = center[k]
            coupled = mix[k][0] * center[0]
            for j in range(1, 5):
                coupled = coupled + mix[k][j] * center[j]
            total = own * q - pull * coupled
            total = total + (x_up * src[k, p + 1] + x_low * src[k, p - 1])
            total = total + (y_up * pltpu.roll(q, rows - 1, 0) + y_low * pltpu.roll(q, 1, 0))
            total = total + (z_up * pltpu.roll(q, lanes - 1, 1) + z_low * pltpu.roll(q, 1, 1))
            if keep:
                total = total + keep * old[k, p]
            dst[k, p] = total
        return carry

    lax.fori_loop(0, hi - lo, body, 0)


def kernel(
    groups, tiles, coupling, basis, snapshots,
    out, coef_out, norm_out,
    held, start, snap, state, one, two, cross, rows_k, spread, left,
    gram_send, gram_all, coef_send, coef_all, norm_send, norm_all,
    load_sem, start_send, start_recv, snap_send, snap_recv,
    gram_ssem, gram_rsem, coef_ssem, coef_rsem, norm_ssem, norm_rsem,
):
    g = lax.axis_index("grp")
    t = lax.axis_index("tile")
    krylov, parts, slab, ny, nz = basis.shape
    local = snapshots.shape[0]
    steps = local * groups
    rim = 3 * steps
    planes = slab + 2 * rim
    near = spans(slab, rim)
    offsets = sorted(near)
    position = krylov - groups + g

    def at(group, offset):
        return {"grp": group, "tile": lax.rem(t + (offset % tiles), tiles)}

    barrier = pltpu.get_barrier_semaphore()

    def greet(r, carry):
        pl.semaphore_signal(barrier, inc=1, device_id=at(g, 0) | {"tile": lax.rem(t + r, tiles)}, device_id_type=MESH)
        return carry

    lax.fori_loop(1, tiles, greet, 0)
    for other in range(1, groups):
        for d in [0] + offsets:
            pl.semaphore_signal(
                barrier, inc=1, device_id=at(lax.rem(g + other, groups), d), device_id_type=MESH
            )

    chunk = 8 if krylov % 8 == 0 else 1
    loads = []
    own = pltpu.make_async_copy(basis.at[position], start.at[:, pl.ds(rim, slab)], load_sem.at[0])
    own.start()
    for n in range(krylov // chunk):
        part = pl.ds(n * chunk, chunk)
        copy = pltpu.make_async_copy(basis.at[part], held.at[part], load_sem.at[1 + n])
        copy.start()
        loads.append(copy)

    pl.semaphore_wait(barrier, tiles - 1 + (groups - 1) * (1 + len(offsets)))

    def target(d, first, last):
        return pl.ds(rim + d * slab + first, last - first)

    start_copies = []
    for n, d in enumerate(offsets):
        first, last = near[d]
        start_copies.append(
            pltpu.make_async_remote_copy(
                src_ref=basis.at[position, :, pl.ds(first, last - first)],
                dst_ref=start.at[:, target(d, first, last)],
                send_sem=start_send.at[n],
                recv_sem=start_recv.at[n],
                device_id=at(g, -d),
                device_id_type=MESH,
            )
        )

    def snap_copy(s, n, d, other):
        first, last = (0, slab) if d == 0 else spans(slab, rim - 3 * s - 1)[d]
        return pltpu.make_async_remote_copy(
            src_ref=snapshots.at[s % local, :, pl.ds(first, last - first)],
            dst_ref=snap.at[s, :, target(d, first, last)],
            send_sem=snap_send.at[s % local, other, n],
            recv_sem=snap_recv.at[s, n],
            device_id=at(lax.rem(g + other, groups), -d),
            device_id_type=MESH,
        )

    def local_snap(s):
        return pltpu.make_async_copy(
            snapshots.at[s % local], snap.at[s, :, pl.ds(rim, slab)], load_sem.at[1 + krylov // chunk + s % local]
        )

    def snap_offsets(s):
        inside = spans(slab, rim - 3 * s - 1)
        return [(n, d) for n, d in enumerate([0] + offsets) if d == 0 or d in inside]

    for copy in start_copies:
        copy.start()
    for s in range(steps):
        @pl.when(g == s // local)
        def _():
            local_snap(s).start()
            for n, d in snap_offsets(s):
                for other in range(groups):
                    if d or other:
                        snap_copy(s, n, d, other).start()

    for copy in loads:
        copy.wait()
    size = krylov * ny
    wide = jnp.concatenate(
        [held[:, c, x].reshape(size, nz) for c in range(parts) for x in range(slab)], axis=1
    )
    cross[...] = lax.dot_general(
        wide, wide, (((1,), (1,)), ((), ())), preferred_element_type=f32
    )
    line = lax.broadcasted_iota(jnp.int32, (size, size), 0)
    column = lax.broadcasted_iota(jnp.int32, (size, size), 1)
    kept = jnp.where(lax.rem(line, ny) == lax.rem(column, ny), cross[...], 0.0)
    kept = jnp.sum(kept.reshape(krylov, ny, size), axis=1)
    pick = (
        lax.broadcasted_iota(jnp.int32, (size, krylov), 0) // ny
        == lax.broadcasted_iota(jnp.int32, (size, krylov), 1)
    ).astype(f32)
    gram_send[...] = jnp.dot(kept, pick, precision=HIGHEST, preferred_element_type=f32)

    def share(send, everyone, ssem, rsem):
        def copy(r):
            return pltpu.make_async_remote_copy(
                src_ref=send,
                dst_ref=everyone.at[t],
                send_sem=ssem.at[r],
                recv_sem=rsem.at[r],
                device_id={"grp": g, "tile": lax.rem(t + r, tiles)},
                device_id_type=MESH,
            )

        def begin():
            lax.fori_loop(1, tiles, lambda r, c: (copy(r).start(), c)[1], 0)
            everyone[t] = send[...]

        def arrive():
            def one_wait(r, c):
                pltpu.make_async_remote_copy(
                    src_ref=send,
                    dst_ref=everyone.at[lax.rem(t - r + tiles, tiles)],
                    send_sem=ssem.at[r],
                    recv_sem=rsem.at[r],
                    device_id={"grp": g, "tile": lax.rem(t + r, tiles)},
                    device_id_type=MESH,
                ).wait_recv()
                return c
            lax.fori_loop(1, tiles, one_wait, 0)

        def drain():
            lax.fori_loop(1, tiles, lambda r, c: (copy(r).wait_send(), c)[1], 0)

        return begin, arrive, drain

    gram_begin, gram_arrive, gram_drain = share(gram_send, gram_all, gram_ssem, gram_rsem)
    coef_begin, coef_arrive, coef_drain = share(coef_send, coef_all, coef_ssem, coef_rsem)
    norm_begin, norm_arrive, norm_drain = share(norm_send, norm_all, norm_ssem, norm_rsem)
    gram_begin()

    own.wait()
    for n, d in enumerate(offsets):
        first, last = near[d]
        pltpu.make_async_remote_copy(
            src_ref=basis.at[position, :, pl.ds(first, last - first)],
            dst_ref=start.at[:, target(d, first, last)],
            send_sem=start_send.at[n],
            recv_sem=start_recv.at[n],
            device_id=at(g, -d),
            device_id_type=MESH,
        ).wait_recv()
    for s in range(steps):
        @pl.when(g == s // local)
        def _():
            local_snap(s).wait()
        if groups > 1:
            @pl.when(g != s // local)
            def _():
                snap_copy(s, 0, 0, 1).wait_recv()
        for n, d in snap_offsets(s):
            if d:
                snap_copy(s, n, d, 1 % groups).wait_recv()

    def widen(p, carry):
        for k in range(parts):
            state[k, p] = start[k, p].astype(f32)
        return carry

    lax.fori_loop(0, planes, widen, 0)
    lo, hi = 0, planes
    for s in range(steps):
        stage(state, state, one, snap, s, coupling, lo + 1, hi - 1, 0.0, 1.0)
        stage(one, state, two, snap, s, coupling, lo + 2, hi - 2, 0.75, 0.25)
        stage(two, state, state, snap, s, coupling, lo + 3, hi - 3, 1.0 / 3.0, 2.0 / 3.0)
        lo, hi = lo + 3, hi - 3

    count = f32(parts * slab * ny * nz * tiles)

    def project(k, carry):
        total = jnp.zeros((ny, nz), f32)
        for c in range(parts):
            for x in range(slab):
                total = total + held[k, c, x].astype(f32) * state[c, rim + x]
        rows_k[pl.ds(k, 1), :] = jnp.sum(total, axis=0, keepdims=True)
        return carry

    lax.fori_loop(0, krylov, project, 0)
    ones = jnp.ones((8, nz), f32)
    inner = lax.dot_general(
        ones, rows_k[...], (((1,), (1,)), ((), ())), precision=HIGHEST, preferred_element_type=f32
    )
    coef_send[...] = inner[0:1]
    coef_begin()
    gram_arrive()
    gram = jnp.sum(gram_all[...], axis=0) / count
    coef_arrive()
    first_coef = jnp.sum(coef_all[...], axis=0) / count
    first_rows = jnp.broadcast_to(first_coef, (8, krylov))
    second_rows = first_rows - jnp.dot(first_rows, gram, precision=HIGHEST, preferred_element_type=f32)
    both = first_rows + second_rows
    coef_out[...] = both[0:1]
    for k in range(krylov):
        spread[k] = jnp.broadcast_to(both[:, k : k + 1], (8, nz))

    def subtract(x, total):
        for c in range(parts):
            value = state[c, rim + x]
            removed = jnp.zeros((ny // 8, 8, nz), f32)
            for k in range(krylov):
                removed = removed + spread[k][None] * held[k, c, x].astype(f32).reshape(ny // 8, 8, nz)
            value = value - removed.reshape(ny, nz)
            left[c, x] = value
            total = total + value * value
        return total

    total = lax.fori_loop(0, slab, subtract, jnp.zeros((ny, nz), f32))
    norm_send[...] = jnp.sum(total, axis=0, keepdims=True)
    norm_begin()
    for copy in start_copies:
        copy.wait_send()
    for s in range(steps):
        @pl.when(g == s // local)
        def _():
            for n, d in snap_offsets(s):
                for other in range(groups):
                    if d or other:
                        snap_copy(s, n, d, other).wait_send()
    gram_drain()
    coef_drain()
    norm_arrive()
    square = jnp.sum(jnp.sum(norm_all[...], axis=0), axis=1, keepdims=True) / count
    norm = jnp.sqrt(square)
    norm_out[...] = jnp.broadcast_to(norm, norm_out.shape)
    inverse = jnp.broadcast_to(1.0 / norm, (ny, nz))
    for c in range(parts):
        for x in range(slab):
            out[0, c, x] = left[c, x] * inverse
    norm_drain()


def on_device(groups, tiles, basis, snapshots, coupling):
    krylov, parts, slab, ny, nz = basis.shape
    local, fields = snapshots.shape[:2]
    steps = local * groups
    rim = 3 * steps
    planes = slab + 2 * rim
    count = len(spans(slab, rim))
    dma = pltpu.SemaphoreType.DMA
    field = pltpu.VMEM((parts, planes, ny, nz), f32)
    whole = pl.BlockSpec(memory_space=pltpu.VMEM)
    new_vector, coefs, norms = pl.pallas_call(
        functools.partial(kernel, groups, tiles),
        name="propagate",
        out_shape=(
            jax.ShapeDtypeStruct((1, parts, slab, ny, nz), f32),
            jax.ShapeDtypeStruct((1, krylov), f32),
            jax.ShapeDtypeStruct((1, nz), f32),
        ),
        in_specs=[
            pl.BlockSpec(memory_space=pltpu.SMEM),
            pl.BlockSpec(memory_space=pl.ANY),
            pl.BlockSpec(memory_space=pl.ANY),
        ],
        out_specs=(whole, whole, whole),
        scratch_shapes=[
            pltpu.VMEM(basis.shape, bf16),
            pltpu.VMEM((parts, planes, ny, nz), bf16),
            pltpu.VMEM((steps, fields, planes, ny, nz), bf16),
            field,
            field,
            field,
            pltpu.VMEM((krylov * ny, krylov * ny), f32),
            pltpu.VMEM((krylov, nz), f32),
            pltpu.VMEM((krylov, 8, nz), f32),
            pltpu.VMEM((parts, slab, ny, nz), f32),
            pltpu.VMEM((krylov, krylov), f32),
            pltpu.VMEM((tiles, krylov, krylov), f32),
            pltpu.VMEM((1, krylov), f32),
            pltpu.VMEM((tiles, 1, krylov), f32),
            pltpu.VMEM((1, nz), f32),
            pltpu.VMEM((tiles, 1, nz), f32),
            dma((1 + krylov + local,)),
            dma((count,)),
            dma((count,)),
            dma((local, groups, count + 1)),
            dma((steps, count + 1)),
            dma((tiles,)),
            dma((tiles,)),
            dma((tiles,)),
            dma((tiles,)),
            dma((tiles,)),
            dma((tiles,)),
        ],
        compiler_params=pltpu.CompilerParams(
            collective_id=0, has_side_effects=True, vmem_limit_bytes=50 * 2**20
        ),
    )(coupling, basis, snapshots)
    return new_vector, coefs, norms[0, :1]


def solution(mesh):
    placed = (P(None, None, "tile", None, None), P("grp", None, "tile", None, None), P())
    return jax.shard_map(
        functools.partial(on_device, mesh.shape["grp"], mesh.shape["tile"]),
        mesh=mesh,
        in_specs=placed,
        out_specs=(P("grp", None, "tile", None, None), P("grp", None), P("grp")),
        check_vma=False,
    )
```

```python
import functools

import jax
import jax.numpy as jnp
from jax import lax
from jax.experimental import pallas as pl
from jax.experimental.pallas import tpu as pltpu
from jax.sharding import PartitionSpec as P

viscosity = 0.5
time_step = 0.3
f32 = jnp.float32
bf16 = jnp.bfloat16
MESH = pl.DeviceIdType.MESH
HIGHEST = lax.Precision.HIGHEST


def spans(slab, rim):
    found = {}
    reach = -(-rim // slab)
    for d in range(1, reach + 1):
        width = min(slab, rim - (d - 1) * slab)
        found[-d] = (slab - width, slab)
        found[d] = (0, width)
    return found


def stage(src, old, dst, snap, step, coupling, lo, hi, keep, gain):
    rows, lanes = src.shape[2], src.shape[3]
    row = lax.broadcasted_iota(jnp.int32, (rows, lanes), 0)
    first = row == 0
    last = row == rows - 1
    step_gain = time_step * gain
    mix = [[coupling[k, j] for j in range(5)] for k in range(5)]

    def body(i, carry):
        p = lo + i
        base = [snap[step, n, p].astype(f32) for n in range(4)]
        half = [(0.5 * step_gain) * base[n] for n in range(3)]
        edge = viscosity * step_gain
        x_up, x_low = edge - half[0], edge + half[0]
        y_up = jnp.where(last, 0.0, edge - half[1])
        y_low = jnp.where(first, 0.0, edge + half[1])
        z_up, z_low = edge - half[2], edge + half[2]
        pull = step_gain * base[3]
        center = [src[k, p] for k in range(5)]
        own = gain - 6.0 * viscosity * step_gain
        for k in range(5):
            q = center[k]
            coupled = mix[k][0] * center[0]
            for j in range(1, 5):
                coupled = coupled + mix[k][j] * center[j]
            total = own * q - pull * coupled
            total = total + (x_up * src[k, p + 1] + x_low * src[k, p - 1])
            total = total + (y_up * pltpu.roll(q, rows - 1, 0) + y_low * pltpu.roll(q, 1, 0))
            total = total + (z_up * pltpu.roll(q, lanes - 1, 1) + z_low * pltpu.roll(q, 1, 1))
            if keep:
                total = total + keep * old[k, p]
            dst[k, p] = total
        return carry

    lax.fori_loop(0, hi - lo, body, 0, unroll=2)


def kernel(
    groups, tiles, coupling, basis, snapshots,
    left, coef_out, square_out,
    held, start, snap, state, one, two, cross, rows_k, spread,
    gram_send, gram_all, coef_send, coef_all, norm_send, norm_all,
    load_sem, start_send, start_recv, snap_send, snap_recv,
    gram_ssem, gram_rsem, coef_ssem, coef_rsem, norm_ssem, norm_rsem,
):
    g = lax.axis_index("grp")
    t = lax.axis_index("tile")
    krylov, parts, slab, ny, nz = basis.shape
    local = snapshots.shape[0]
    steps = local * groups
    rim = 3 * steps
    planes = slab + 2 * rim
    near = spans(slab, rim)
    offsets = sorted(near)
    position = krylov - groups + g

    def at(group, offset):
        return {"grp": group, "tile": lax.rem(t + (offset % tiles), tiles)}

    barrier = pltpu.get_barrier_semaphore()

    def greet(r, carry):
        pl.semaphore_signal(barrier, inc=1, device_id=at(g, 0) | {"tile": lax.rem(t + r, tiles)}, device_id_type=MESH)
        return carry

    lax.fori_loop(1, tiles, greet, 0)
    for other in range(1, groups):
        pl.semaphore_signal(
            barrier, inc=1, device_id=at(lax.rem(g + other, groups), 0), device_id_type=MESH
        )

    chunk = 8 if krylov % 8 == 0 else 1
    loads = []
    own = pltpu.make_async_copy(basis.at[position], start.at[:, pl.ds(rim, slab)], load_sem.at[0])
    own.start()
    for n in range(krylov // chunk):
        part = pl.ds(n * chunk, chunk)
        copy = pltpu.make_async_copy(basis.at[part], held.at[part], load_sem.at[1 + n])
        copy.start()
        loads.append(copy)

    for copy in loads:
        copy.wait()
    size = krylov * ny
    wide = jnp.concatenate(
        [held[:, c, x].reshape(size, nz) for c in range(parts) for x in range(slab)], axis=1
    )
    cross[...] = lax.dot_general(
        wide, wide, (((1,), (1,)), ((), ())), preferred_element_type=f32
    )
    line = lax.broadcasted_iota(jnp.int32, (size, size), 0)
    column = lax.broadcasted_iota(jnp.int32, (size, size), 1)
    kept = jnp.where(lax.rem(line, ny) == lax.rem(column, ny), cross[...], 0.0)
    kept = jnp.sum(kept.reshape(krylov, ny, size), axis=1)
    pick = (
        lax.broadcasted_iota(jnp.int32, (size, krylov), 0) // ny
        == lax.broadcasted_iota(jnp.int32, (size, krylov), 1)
    ).astype(f32)
    gram_send[...] = jnp.dot(kept, pick, precision=HIGHEST, preferred_element_type=f32)

    pl.semaphore_wait(barrier, tiles - 1 + groups - 1)

    def target(d, first, last):
        return pl.ds(rim + d * slab + first, last - first)

    start_copies = []
    for n, d in enumerate(offsets):
        first, last = near[d]
        start_copies.append(
            pltpu.make_async_remote_copy(
                src_ref=basis.at[position, :, pl.ds(first, last - first)],
                dst_ref=start.at[:, target(d, first, last)],
                send_sem=start_send.at[n],
                recv_sem=start_recv.at[n],
                device_id=at(g, -d),
                device_id_type=MESH,
            )
        )

    def snap_copy(s, n, d, other):
        first, last = (0, slab) if d == 0 else spans(slab, rim - 3 * s - 1)[d]
        return pltpu.make_async_remote_copy(
            src_ref=snapshots.at[s % local, :, pl.ds(first, last - first)],
            dst_ref=snap.at[s, :, target(d, first, last)],
            send_sem=snap_send.at[s % local, other, n],
            recv_sem=snap_recv.at[s, n],
            device_id=at(lax.rem(g + other, groups), -d),
            device_id_type=MESH,
        )

    def local_snap(s):
        return pltpu.make_async_copy(
            snapshots.at[s % local], snap.at[s, :, pl.ds(rim, slab)], load_sem.at[1 + krylov // chunk + s % local]
        )

    def snap_offsets(s):
        inside = spans(slab, rim - 3 * s - 1)
        return [(n, d) for n, d in enumerate([0] + offsets) if d == 0 or d in inside]

    def send_snap(s):
        @pl.when(g == s // local)
        def _():
            local_snap(s).start()
            for n, d in snap_offsets(s):
                for other in range(1 if d else groups):
                    if d or other:
                        snap_copy(s, n, d, other).start()

    def relay_copy(s, n, d, other):
        first, last = spans(slab, rim - 3 * s - 1)[d]
        cells = snap.at[s, :, target(d, first, last)]
        return pltpu.make_async_remote_copy(
            src_ref=cells,
            dst_ref=cells,
            send_sem=snap_send.at[s % local, other, n],
            recv_sem=snap_recv.at[s, n],
            device_id=at(lax.rem(g + other, groups), 0),
            device_id_type=MESH,
        )

    def relay(s):
        @pl.when(g == s // local)
        def _():
            for n, d in snap_offsets(s):
                if d:
                    snap_copy(s, n, d, 0).wait_recv()
                    for other in range(1, groups):
                        relay_copy(s, n, d, other).start()
            local_snap(s).wait()

    def receive(s):
        if groups > 1:
            @pl.when(g != s // local)
            def _():
                snap_copy(s, 0, 0, 1).wait_recv()
                for n, d in snap_offsets(s):
                    if d:
                        relay_copy(s, n, d, 1).wait_recv()

    for s in range(local):
        send_snap(s)
    for copy in start_copies:
        copy.start()
    for s in range(local, steps):
        send_snap(s)

    def share(send, everyone, ssem, rsem):
        def copy(r):
            return pltpu.make_async_remote_copy(
                src_ref=send,
                dst_ref=everyone.at[t],
                send_sem=ssem.at[r],
                recv_sem=rsem.at[r],
                device_id={"grp": g, "tile": lax.rem(t + r, tiles)},
                device_id_type=MESH,
            )

        def begin():
            lax.fori_loop(1, tiles, lambda r, c: (copy(r).start(), c)[1], 0)
            everyone[t] = send[...]

        def arrive():
            def one_wait(r, c):
                pltpu.make_async_remote_copy(
                    src_ref=send,
                    dst_ref=everyone.at[lax.rem(t - r + tiles, tiles)],
                    send_sem=ssem.at[r],
                    recv_sem=rsem.at[r],
                    device_id={"grp": g, "tile": lax.rem(t + r, tiles)},
                    device_id_type=MESH,
                ).wait_recv()
                return c
            lax.fori_loop(1, tiles, one_wait, 0)

        def drain():
            lax.fori_loop(1, tiles, lambda r, c: (copy(r).wait_send(), c)[1], 0)

        return begin, arrive, drain

    gram_begin, gram_arrive, gram_drain = share(gram_send, gram_all, gram_ssem, gram_rsem)
    coef_begin, coef_arrive, coef_drain = share(coef_send, coef_all, coef_ssem, coef_rsem)
    norm_begin, norm_arrive, norm_drain = share(norm_send, norm_all, norm_ssem, norm_rsem)
    gram_begin()

    relay(0)
    own.wait()
    for copy in start_copies:
        copy.wait_recv()

    def widen(p, carry):
        for k in range(parts):
            state[k, p] = start[k, p].astype(f32)
        return carry

    lax.fori_loop(0, planes, widen, 0)
    lo, hi = 0, planes
    for s in range(steps):
        receive(s)
        stage(state, state, one, snap, s, coupling, lo + 1, hi - 1, 0.0, 1.0)
        if s == 0:
            for later in range(1, steps):
                relay(later)
        stage(one, state, two, snap, s, coupling, lo + 2, hi - 2, 0.75, 0.25)
        stage(two, state, state, snap, s, coupling, lo + 3, hi - 3, 1.0 / 3.0, 2.0 / 3.0)
        lo, hi = lo + 3, hi - 3

    count = f32(parts * slab * ny * nz * tiles)

    def project(k, carry):
        total = jnp.zeros((ny, nz), f32)
        for c in range(parts):
            for x in range(slab):
                total = total + held[k, c, x].astype(f32) * state[c, rim + x]
        rows_k[pl.ds(k, 1), :] = jnp.sum(total, axis=0, keepdims=True)
        return carry

    lax.fori_loop(0, krylov, project, 0, unroll=4)
    ones = jnp.ones((8, nz), f32)
    inner = lax.dot_general(
        ones, rows_k[...], (((1,), (1,)), ((), ())), precision=HIGHEST, preferred_element_type=f32
    )
    coef_send[...] = inner[0:1]
    coef_begin()
    gram_arrive()
    gram = jnp.sum(gram_all[...], axis=0) / count
    coef_arrive()
    first_coef = jnp.sum(coef_all[...], axis=0) / count
    first_rows = jnp.broadcast_to(first_coef, (8, krylov))
    second_rows = first_rows - jnp.dot(first_rows, gram, precision=HIGHEST, preferred_element_type=f32)
    both = first_rows + second_rows
    coef_out[...] = both[0:1]
    for k in range(krylov):
        spread[k] = jnp.broadcast_to(both[:, k : k + 1], (8, nz))

    def subtract(x, total):
        for c in range(parts):
            value = state[c, rim + x]
            removed = jnp.zeros((ny // 8, 8, nz), f32)
            for k in range(krylov):
                removed = removed + spread[k][None] * held[k, c, x].astype(f32).reshape(ny // 8, 8, nz)
            value = value - removed.reshape(ny, nz)
            left[0, c, x] = value
            total = total + value * value
        return total

    total = lax.fori_loop(0, slab, subtract, jnp.zeros((ny, nz), f32))
    norm_send[...] = jnp.sum(total, axis=0, keepdims=True)
    norm_begin()
    for copy in start_copies:
        copy.wait_send()
    for s in range(steps):
        @pl.when(g == s // local)
        def _():
            for n, d in snap_offsets(s):
                for other in range(groups):
                    if d and other:
                        relay_copy(s, n, d, other).wait_send()
                    elif d or other:
                        snap_copy(s, n, d, other).wait_send()
    gram_drain()
    coef_drain()
    norm_arrive()
    square = jnp.sum(jnp.sum(norm_all[...], axis=0), axis=1, keepdims=True) / count
    square_out[...] = jnp.broadcast_to(square, square_out.shape)
    norm_drain()


def finish(left, coefs, square, out, coef_out, norm_out):
    norm = jnp.sqrt(square[...])
    norm_out[...] = norm
    coef_out[...] = coefs[...]
    inverse = jnp.broadcast_to(1.0 / norm, left.shape[3:])
    for c in range(left.shape[1]):
        for x in range(left.shape[2]):
            out[0, c, x] = left[0, c, x] * inverse


def on_device(groups, tiles, basis, snapshots, coupling):
    krylov, parts, slab, ny, nz = basis.shape
    local, fields = snapshots.shape[:2]
    steps = local * groups
    rim = 3 * steps
    planes = slab + 2 * rim
    count = len(spans(slab, rim))
    dma = pltpu.SemaphoreType.DMA
    field = pltpu.VMEM((parts, planes, ny, nz), f32)
    whole = pl.BlockSpec(memory_space=pltpu.VMEM)
    results = pl.pallas_call(
        functools.partial(kernel, groups, tiles),
        name="propagate",
        out_shape=(
            jax.ShapeDtypeStruct((1, parts, slab, ny, nz), f32),
            jax.ShapeDtypeStruct((1, krylov), f32),
            jax.ShapeDtypeStruct((1, nz), f32),
        ),
        in_specs=[
            pl.BlockSpec(memory_space=pltpu.SMEM),
            pl.BlockSpec(memory_space=pl.ANY),
            pl.BlockSpec(memory_space=pl.ANY),
        ],
        out_specs=(whole, whole, whole),
        scratch_shapes=[
            pltpu.VMEM(basis.shape, bf16),
            pltpu.VMEM((parts, planes, ny, nz), bf16),
            pltpu.VMEM((steps, fields, planes, ny, nz), bf16),
            field,
            field,
            field,
            pltpu.VMEM((krylov * ny, krylov * ny), f32),
            pltpu.VMEM((krylov, nz), f32),
            pltpu.VMEM((krylov, 8, nz), f32),
            pltpu.VMEM((krylov, krylov), f32),
            pltpu.VMEM((tiles, krylov, krylov), f32),
            pltpu.VMEM((1, krylov), f32),
            pltpu.VMEM((tiles, 1, krylov), f32),
            pltpu.VMEM((1, nz), f32),
            pltpu.VMEM((tiles, 1, nz), f32),
            dma((1 + krylov + local,)),
            dma((count,)),
            dma((count,)),
            dma((local, groups, count + 1)),
            dma((steps, count + 1)),
            dma((tiles,)),
            dma((tiles,)),
            dma((tiles,)),
            dma((tiles,)),
            dma((tiles,)),
            dma((tiles,)),
        ],
        compiler_params=pltpu.CompilerParams(
            collective_id=0, has_side_effects=True, vmem_limit_bytes=67043328
        ),
    )(coupling, basis, snapshots)
    new_vector, coefs, norms = pl.pallas_call(
        finish,
        name="finish",
        out_shape=tuple(jax.ShapeDtypeStruct(a.shape, f32) for a in results),
        in_specs=[whole] * 3,
        out_specs=(whole, whole, whole),
    )(*results)
    return new_vector, coefs, norms[0, :1]


def solution(mesh):
    placed = (P(None, None, "tile", None, None), P("grp", None, "tile", None, None), P())
    return jax.shard_map(
        functools.partial(on_device, mesh.shape["grp"], mesh.shape["tile"]),
        mesh=mesh,
        in_specs=placed,
        out_specs=(P("grp", None, "tile", None, None), P("grp", None), P("grp")),
        check_vma=False,
    )
```

```python
import functools

import jax
import jax.numpy as jnp
from jax import lax
from jax.experimental import pallas as pl
from jax.experimental.pallas import tpu as pltpu
from jax.sharding import PartitionSpec as P

viscosity = 0.5
time_step = 0.3
f32 = jnp.float32
bf16 = jnp.bfloat16
MESH = pl.DeviceIdType.MESH
HIGHEST = lax.Precision.HIGHEST


def spans(slab, rim):
    found = {}
    reach = -(-rim // slab)
    for d in range(1, reach + 1):
        width = min(slab, rim - (d - 1) * slab)
        found[-d] = (slab - width, slab)
        found[d] = (0, width)
    return found


def gram_blocks(krylov, lanes):
    blocks = max(lanes // krylov, 1)
    return (blocks, krylov // blocks) if krylov % (8 * blocks) == 0 else (1, krylov)


def stage(src, old, dst, snap, step, coupling, lo, hi, keep, gain):
    rows, lanes = src.shape[2], src.shape[3]
    row = lax.broadcasted_iota(jnp.int32, (rows, lanes), 0)
    first = row == 0
    last = row == rows - 1
    step_gain = time_step * gain
    mix = [[coupling[k, j] for j in range(5)] for k in range(5)]

    def body(i, carry):
        p = lo + i
        base = [snap[step, n, p].astype(f32) for n in range(4)]
        half = [(0.5 * step_gain) * base[n] for n in range(3)]
        edge = viscosity * step_gain
        x_up, x_low = edge - half[0], edge + half[0]
        y_up = jnp.where(last, 0.0, edge - half[1])
        y_low = jnp.where(first, 0.0, edge + half[1])
        z_up, z_low = edge - half[2], edge + half[2]
        pull = step_gain * base[3]
        center = [src[k, p] for k in range(5)]
        own = gain - 6.0 * viscosity * step_gain
        for k in range(5):
            q = center[k]
            coupled = mix[k][0] * center[0]
            for j in range(1, 5):
                coupled = coupled + mix[k][j] * center[j]
            total = own * q - pull * coupled
            total = total + (x_up * src[k, p + 1] + x_low * src[k, p - 1])
            total = total + (y_up * pltpu.roll(q, rows - 1, 0) + y_low * pltpu.roll(q, 1, 0))
            total = total + (z_up * pltpu.roll(q, lanes - 1, 1) + z_low * pltpu.roll(q, 1, 1))
            if keep:
                total = total + keep * old[k, p]
            dst[k, p] = total
        return carry

    lax.fori_loop(0, hi - lo, body, 0, unroll=4)


def kernel(
    groups, tiles, coupling, basis, snapshots,
    left, coef_out, square_out,
    held, start, snap, state, one, two, cross, rows_k, spread,
    gram_send, gram_all, coef_send, coef_all, norm_send, norm_all,
    load_sem, start_send, start_recv, snap_send, snap_recv,
    gram_ssem, gram_rsem, coef_ssem, coef_rsem, norm_ssem, norm_rsem,
):
    g = lax.axis_index("grp")
    t = lax.axis_index("tile")
    krylov, parts, slab, ny, nz = basis.shape
    local = snapshots.shape[0]
    steps = local * groups
    rim = 3 * steps
    planes = slab + 2 * rim
    near = spans(slab, rim)
    offsets = sorted(near)
    position = krylov - groups + g

    def at(group, offset):
        return {"grp": group, "tile": lax.rem(t + (offset % tiles), tiles)}

    barrier = pltpu.get_barrier_semaphore()

    def greet(r, carry):
        pl.semaphore_signal(barrier, inc=1, device_id=at(g, 0) | {"tile": lax.rem(t + r, tiles)}, device_id_type=MESH)
        return carry

    lax.fori_loop(1, tiles, greet, 0)
    for other in range(1, groups):
        pl.semaphore_signal(
            barrier, inc=1, device_id=at(lax.rem(g + other, groups), 0), device_id_type=MESH
        )

    chunk = 8 if krylov % 8 == 0 else 1
    loads = []
    own = pltpu.make_async_copy(basis.at[position], start.at[:, pl.ds(rim, slab)], load_sem.at[0])
    own.start()
    for n in range(krylov // chunk):
        part = pl.ds(n * chunk, chunk)
        copy = pltpu.make_async_copy(basis.at[part], held.at[part], load_sem.at[1 + n])
        copy.start()
        loads.append(copy)

    for copy in loads:
        copy.wait()
    size = krylov * ny
    wide = jnp.concatenate(
        [held[:, c, x].reshape(size, nz) for c in range(parts) for x in range(slab)], axis=1
    )
    cross[...] = lax.dot_general(
        wide, wide, (((1,), (1,)), ((), ())), preferred_element_type=f32
    )
    line = lax.broadcasted_iota(jnp.int32, (size, size), 0)
    column = lax.broadcasted_iota(jnp.int32, (size, size), 1)
    kept = jnp.where(lax.rem(line, ny) == lax.rem(column, ny), cross[...], 0.0)
    kept = jnp.sum(kept.reshape(krylov, ny, size), axis=1)
    pick = (
        lax.broadcasted_iota(jnp.int32, (size, krylov), 0) // ny
        == lax.broadcasted_iota(jnp.int32, (size, krylov), 1)
    ).astype(f32)
    gram = jnp.dot(kept, pick, precision=HIGHEST, preferred_element_type=f32)
    blocks, height = gram_blocks(krylov, nz)
    gram_send[...] = jnp.concatenate(
        [gram[n * height : (n + 1) * height] for n in range(blocks)], axis=1
    )

    pl.semaphore_wait(barrier, tiles - 1 + groups - 1)

    def target(d, first, last):
        return pl.ds(rim + d * slab + first, last - first)

    start_copies = []
    for n, d in enumerate(offsets):
        first, last = near[d]
        start_copies.append(
            pltpu.make_async_remote_copy(
                src_ref=basis.at[position, :, pl.ds(first, last - first)],
                dst_ref=start.at[:, target(d, first, last)],
                send_sem=start_send.at[n],
                recv_sem=start_recv.at[n],
                device_id=at(g, -d),
                device_id_type=MESH,
            )
        )

    def snap_copy(s, n, d, other):
        first, last = (0, slab) if d == 0 else spans(slab, rim - 3 * s - 1)[d]
        return pltpu.make_async_remote_copy(
            src_ref=snapshots.at[s % local, :, pl.ds(first, last - first)],
            dst_ref=snap.at[s, :, target(d, first, last)],
            send_sem=snap_send.at[s % local, other, n],
            recv_sem=snap_recv.at[s, n],
            device_id=at(lax.rem(g + other, groups), -d),
            device_id_type=MESH,
        )

    def local_snap(s):
        return pltpu.make_async_copy(
            snapshots.at[s % local], snap.at[s, :, pl.ds(rim, slab)], load_sem.at[1 + krylov // chunk + s % local]
        )

    def snap_offsets(s):
        inside = spans(slab, rim - 3 * s - 1)
        return [(n, d) for n, d in enumerate([0] + offsets) if d == 0 or d in inside]

    def send_snap(s):
        @pl.when(g == s // local)
        def _():
            local_snap(s).start()
            for n, d in snap_offsets(s):
                for other in range(1 if d else groups):
                    if d or other:
                        snap_copy(s, n, d, other).start()

    def relay_copy(s, n, d, other):
        first, last = spans(slab, rim - 3 * s - 1)[d]
        cells = snap.at[s, :, target(d, first, last)]
        return pltpu.make_async_remote_copy(
            src_ref=cells,
            dst_ref=cells,
            send_sem=snap_send.at[s % local, other, n],
            recv_sem=snap_recv.at[s, n],
            device_id=at(lax.rem(g + other, groups), 0),
            device_id_type=MESH,
        )

    def relay(s):
        @pl.when(g == s // local)
        def _():
            for n, d in snap_offsets(s):
                if d:
                    snap_copy(s, n, d, 0).wait_recv()
                    for other in range(1, groups):
                        relay_copy(s, n, d, other).start()
            local_snap(s).wait()

    def receive(s):
        if groups > 1:
            @pl.when(g != s // local)
            def _():
                snap_copy(s, 0, 0, 1).wait_recv()
                for n, d in snap_offsets(s):
                    if d:
                        relay_copy(s, n, d, 1).wait_recv()

    for s in range(local):
        send_snap(s)
    for copy in start_copies:
        copy.start()
    for s in range(local, steps):
        send_snap(s)

    def share(send, everyone, ssem, rsem):
        def copy(r):
            return pltpu.make_async_remote_copy(
                src_ref=send,
                dst_ref=everyone.at[t],
                send_sem=ssem.at[r],
                recv_sem=rsem.at[r],
                device_id={"grp": g, "tile": lax.rem(t + r, tiles)},
                device_id_type=MESH,
            )

        def begin():
            lax.fori_loop(1, tiles, lambda r, c: (copy(r).start(), c)[1], 0)
            everyone[t] = send[...]

        def arrive():
            def one_wait(r, c):
                pltpu.make_async_remote_copy(
                    src_ref=send,
                    dst_ref=everyone.at[lax.rem(t - r + tiles, tiles)],
                    send_sem=ssem.at[r],
                    recv_sem=rsem.at[r],
                    device_id={"grp": g, "tile": lax.rem(t + r, tiles)},
                    device_id_type=MESH,
                ).wait_recv()
                return c
            lax.fori_loop(1, tiles, one_wait, 0)

        def drain():
            lax.fori_loop(1, tiles, lambda r, c: (copy(r).wait_send(), c)[1], 0)

        return begin, arrive, drain

    gram_begin, gram_arrive, gram_drain = share(gram_send, gram_all, gram_ssem, gram_rsem)
    coef_begin, coef_arrive, coef_drain = share(coef_send, coef_all, coef_ssem, coef_rsem)
    norm_begin, norm_arrive, norm_drain = share(norm_send, norm_all, norm_ssem, norm_rsem)
    gram_begin()

    relay(0)
    own.wait()
    for copy in start_copies:
        copy.wait_recv()

    def widen(p, carry):
        for k in range(parts):
            state[k, p] = start[k, p].astype(f32)
        return carry

    lax.fori_loop(0, planes, widen, 0)
    lo, hi = 0, planes
    for s in range(steps):
        receive(s)
        stage(state, state, one, snap, s, coupling, lo + 1, hi - 1, 0.0, 1.0)
        if s == 0:
            for later in range(1, steps):
                relay(later)
        stage(one, state, two, snap, s, coupling, lo + 2, hi - 2, 0.75, 0.25)
        stage(two, state, state, snap, s, coupling, lo + 3, hi - 3, 1.0 / 3.0, 2.0 / 3.0)
        lo, hi = lo + 3, hi - 3

    count = f32(parts * slab * ny * nz * tiles)

    def project(k, carry):
        total = jnp.zeros((ny, nz), f32)
        for c in range(parts):
            for x in range(slab):
                total = total + held[k, c, x].astype(f32) * state[c, rim + x]
        rows_k[pl.ds(k, 1), :] = jnp.sum(total, axis=0, keepdims=True)
        return carry

    lax.fori_loop(0, krylov, project, 0, unroll=4)
    ones = jnp.ones((8, nz), f32)
    inner = lax.dot_general(
        ones, rows_k[...], (((1,), (1,)), ((), ())), precision=HIGHEST, preferred_element_type=f32
    )
    coef_send[...] = inner[0:1]
    coef_begin()
    gram_arrive()
    packed = jnp.sum(gram_all[...], axis=0) / count
    gram = jnp.concatenate(
        [packed[:, n * krylov : (n + 1) * krylov] for n in range(blocks)], axis=0
    )
    coef_arrive()
    first_coef = jnp.sum(coef_all[...], axis=0) / count
    first_rows = jnp.broadcast_to(first_coef, (8, krylov))
    second_rows = first_rows - jnp.dot(first_rows, gram, precision=HIGHEST, preferred_element_type=f32)
    both = first_rows + second_rows
    coef_out[...] = both[0:1]
    for k in range(krylov):
        spread[k] = jnp.broadcast_to(both[:, k : k + 1], (8, nz))

    def subtract(x, total):
        for c in range(parts):
            value = state[c, rim + x]
            removed = jnp.zeros((ny // 8, 8, nz), f32)
            for k in range(krylov):
                removed = removed + spread[k][None] * held[k, c, x].astype(f32).reshape(ny // 8, 8, nz)
            value = value - removed.reshape(ny, nz)
            left[0, c, x] = value
            total = total + value * value
        return total

    total = lax.fori_loop(0, slab, subtract, jnp.zeros((ny, nz), f32))
    norm_send[...] = jnp.sum(total, axis=0, keepdims=True)
    norm_begin()
    for copy in start_copies:
        copy.wait_send()
    for s in range(steps):
        @pl.when(g == s // local)
        def _():
            for n, d in snap_offsets(s):
                for other in range(groups):
                    if d and other:
                        relay_copy(s, n, d, other).wait_send()
                    elif d or other:
                        snap_copy(s, n, d, other).wait_send()
    gram_drain()
    coef_drain()
    norm_arrive()
    square = jnp.sum(jnp.sum(norm_all[...], axis=0), axis=1, keepdims=True) / count
    square_out[...] = jnp.broadcast_to(square, square_out.shape)
    norm_drain()


def finish(left, coefs, square, out, coef_out, norm_out):
    norm = jnp.sqrt(square[...])
    norm_out[...] = norm
    coef_out[...] = coefs[...]
    inverse = jnp.broadcast_to(1.0 / norm, left.shape[3:])
    for c in range(left.shape[1]):
        for x in range(left.shape[2]):
            out[0, c, x] = left[0, c, x] * inverse


def on_device(groups, tiles, basis, snapshots, coupling):
    krylov, parts, slab, ny, nz = basis.shape
    local, fields = snapshots.shape[:2]
    steps = local * groups
    rim = 3 * steps
    planes = slab + 2 * rim
    count = len(spans(slab, rim))
    blocks, height = gram_blocks(krylov, nz)
    dma = pltpu.SemaphoreType.DMA
    field = pltpu.VMEM((parts, planes, ny, nz), f32)
    whole = pl.BlockSpec(memory_space=pltpu.VMEM)
    results = pl.pallas_call(
        functools.partial(kernel, groups, tiles),
        name="propagate",
        out_shape=(
            jax.ShapeDtypeStruct((1, parts, slab, ny, nz), f32),
            jax.ShapeDtypeStruct((1, krylov), f32),
            jax.ShapeDtypeStruct((1, nz), f32),
        ),
        in_specs=[
            pl.BlockSpec(memory_space=pltpu.SMEM),
            pl.BlockSpec(memory_space=pl.ANY),
            pl.BlockSpec(memory_space=pl.ANY),
        ],
        out_specs=(whole, whole, whole),
        scratch_shapes=[
            pltpu.VMEM(basis.shape, bf16),
            pltpu.VMEM((parts, planes, ny, nz), bf16),
            pltpu.VMEM((steps, fields, planes, ny, nz), bf16),
            field,
            field,
            field,
            pltpu.VMEM((krylov * ny, krylov * ny), f32),
            pltpu.VMEM((krylov, nz), f32),
            pltpu.VMEM((krylov, 8, nz), f32),
            pltpu.VMEM((height, blocks * krylov), f32),
            pltpu.VMEM((tiles, height, blocks * krylov), f32),
            pltpu.VMEM((1, krylov), f32),
            pltpu.VMEM((tiles, 1, krylov), f32),
            pltpu.VMEM((1, nz), f32),
            pltpu.VMEM((tiles, 1, nz), f32),
            dma((1 + krylov + local,)),
            dma((count,)),
            dma((count,)),
            dma((local, groups, count + 1)),
            dma((steps, count + 1)),
            dma((tiles,)),
            dma((tiles,)),
            dma((tiles,)),
            dma((tiles,)),
            dma((tiles,)),
            dma((tiles,)),
        ],
        compiler_params=pltpu.CompilerParams(
            collective_id=0, has_side_effects=True, vmem_limit_bytes=67043328
        ),
    )(coupling, basis, snapshots)
    new_vector, coefs, norms = pl.pallas_call(
        finish,
        name="finish",
        out_shape=tuple(jax.ShapeDtypeStruct(a.shape, f32) for a in results),
        in_specs=[whole] * 3,
        out_specs=(whole, whole, whole),
    )(*results)
    return new_vector, coefs, norms[0, :1]


def solution(mesh):
    placed = (P(None, None, "tile", None, None), P("grp", None, "tile", None, None), P())
    return jax.shard_map(
        functools.partial(on_device, mesh.shape["grp"], mesh.shape["tile"]),
        mesh=mesh,
        in_specs=placed,
        out_specs=(P("grp", None, "tile", None, None), P("grp", None), P("grp")),
        check_vma=False,
    )
```
